32 devices in a mesh: row: 4 (over x, core), col: 8 (over z, y).
Axes of the slice: x: 2, y: 2, z: 4, core: 2. Of those that a mesh axis runs over, the one named last changes fastest.
Arguments:
- centres: float32 [65536, 64], P(('row', 'col')), may hold values from -6 to 6
- weights: float32 [65536, 64], P(('row', 'col')), may hold values from -0.25 to 0.25
- targets: float32 [512, 64], replicated, may hold values from -6 to 6
- batch_index: int32 [512], replicated, may hold values from 0 to 65535
- nystrom_index: int32 [4096], replicated, may hold values from 0 to 65535
- eigvecs: float32 [4096, 1024], P('row', 'col'), may hold values from -0.09375 to 0.09375
- mode_scale: float32 [1024], P('col'), may hold values from 0.02 to 0.2
Outputs:
- residual: float32 [512, 64], replicated
- step: float32 [65536, 64], P(('row', 'col'))
The draws below stay inside these ranges and needn't reach their ends.
All inputs are finite; a program needn't handle non-finite values.
Results may differ from the reference program's by a relative error of at most 0.0001.
Values sent between devices are 32-bit elements; how exact they have to be, the bound alone decides.
A program may use at most 128 MiB of HBM per device.

```python
import math
import jax
import jax.numpy as jnp
from jax import lax

F = 64
O = 64
M = 4096
Q = 1024
B = 512
P_DEV = 2048
CENTRES = 65536


def set_ends(result, stream_key, least, top_value):
    shape = result.shape
    spot = [jax.random.randint(jax.random.fold_in(stream_key, axis), (), 0, shape[axis]) for axis in range(len(shape))]
    result = result.at[tuple(spot)].set(least)
    longest = shape.index(max(shape))
    spot[longest] = (spot[longest] + 1) % shape[longest]
    return result.at[tuple(spot)].set(top_value)


def level_of(key, dims, cuts, low, top_value):
    def one(axis_at, parts):
        steps = jax.random.uniform(jax.random.fold_in(jax.random.fold_in(key, 6), axis_at), (parts,), jnp.float32, low / len(cuts), top_value / len(cuts))
        return jnp.repeat(jnp.exp(steps), dims[axis_at] // parts).reshape((-1,) + (1,) * (len(dims) - axis_at - 1))

    level = one(*cuts[0])
    for cut in cuts[1:]:
        level = level * one(*cut)
    return level


def gaussian(key, shape, deviation, reach, pieces=(), dtype=jnp.bfloat16):
    result = deviation * jax.random.normal(key, shape, jnp.float32)
    if pieces:
        result = result * level_of(key, shape, pieces, -0.22, 0.18)
    return jnp.clip(result, -reach, reach).astype(dtype)


def setup_inputs(seed: int = 0) -> dict:
    streams_of = jax.random.split(jax.random.key(seed), 8)
    centres = gaussian(streams_of[0], (CENTRES, F), 1.0, 6.0, ((0, 32),), jnp.float32)
    weights = gaussian(streams_of[1], (CENTRES, O), (4.0 / CENTRES ** 0.5), 0.25, ((0, 32),), jnp.float32)
    targets = gaussian(streams_of[2], (B, O), 1.0, 6.0, (), jnp.float32)
    batch_index = set_ends(jax.random.randint(streams_of[3], (B,), 0, CENTRES), jax.random.fold_in(streams_of[3], 1), 0, CENTRES - 1).astype(jnp.int32)
    nystrom_index = set_ends(jax.random.randint(streams_of[4], (M,), 0, CENTRES), jax.random.fold_in(streams_of[4], 1), 0, CENTRES - 1).astype(jnp.int32)
    eigvecs = gaussian(streams_of[5], (M, Q), M ** -0.5, 0.09375, ((0, 4), (1, 8)), jnp.float32)
    mode_scale = jnp.clip(jnp.exp(math.log(0.2) - 2.3025851 * jax.random.uniform(streams_of[6], (Q,), jnp.float32) ** level_of(streams_of[6], (Q,), ((0, 8),), -0.2, 0.2)), 0.02, 0.2)
    return {"centres": centres, "weights": weights, "targets": targets, "batch_index": batch_index, "nystrom_index": nystrom_index, "eigvecs": eigvecs, "mode_scale": mode_scale}


learning_rate = 0.25


def kernel(left, right):
    left_sq = jnp.sum(left * left, axis=1)
    right_sq = jnp.sum(right * right, axis=1)
    inner_prod = jnp.dot(left, right.T, precision=lax.Precision.HIGHEST, preferred_element_type=jnp.float32)
    return jnp.exp(-(left_sq[:, None] + right_sq[None, :] - 2.0 * inner_prod) / float(F))


def reference(centres, weights, targets, batch_index, nystrom_index, eigvecs, mode_scale):
    batch_feats = centres[batch_index]
    nystrom = centres[nystrom_index]
    blocks = CENTRES // P_DEV
    cent_blocks = centres.reshape(blocks, P_DEV, F)
    wts_blocks = weights.reshape(blocks, P_DEV, O)

    def add_block(running, pair):
        cent_blk, wts_blk = pair
        kern_tile = kernel(cent_blk, batch_feats)
        return running + jnp.dot(kern_tile.T, wts_blk, precision=lax.Precision.HIGHEST, preferred_element_type=jnp.float32), None

    prediction, unused = lax.scan(add_block, jnp.zeros((B, O), jnp.float32), (cent_blocks, wts_blocks))
    residual = prediction - targets
    gradient = jnp.dot(kernel(nystrom, batch_feats), residual, precision=lax.Precision.HIGHEST, preferred_element_type=jnp.float32)
    coeff = mode_scale[:, None] * jnp.dot(eigvecs.T, gradient, precision=lax.Precision.HIGHEST, preferred_element_type=jnp.float32)
    correction = jnp.dot(eigvecs, coeff, precision=lax.Precision.HIGHEST, preferred_element_type=jnp.float32)

    def step_block(cent_blk):
        direct = jnp.dot(kernel(cent_blk, batch_feats), residual, precision=lax.Precision.HIGHEST, preferred_element_type=jnp.float32)
        back = jnp.dot(kernel(cent_blk, nystrom), correction, precision=lax.Precision.HIGHEST, preferred_element_type=jnp.float32)
        return learning_rate * (direct - back)

    step = lax.map(step_block, cent_blocks).reshape(CENTRES, O)
    return residual, step
```

```python
import functools
import math

import jax
import jax.numpy as jnp
from jax import lax
from jax.experimental import pallas as pl
from jax.experimental.pallas import tpu as pltpu
from jax.sharding import PartitionSpec as P

learning_rate = 0.25
CORES = 2
MESH = pl.DeviceIdType.MESH
VMEM = pl.BlockSpec(memory_space=pltpu.VMEM)
BF16 = jnp.bfloat16
F32 = jnp.float32


def pieces(value, count):
    parts = []
    for step in range(count):
        part = lax.reduce_precision(value, 8, 7)
        parts.append(part.astype(BF16))
        value = value - part
    return parts


def augmented(feats, left):
    rows, width = feats.shape
    unit = math.log2(math.e) / width
    square = pieces(-unit * jnp.sum(feats * feats, axis=1, keepdims=True), 3)
    ones = [jnp.ones((rows, 3), BF16)]
    if left:
        high, low = pieces(feats * (2.0 * unit), 2)
        parts = [high, low, high] + square + ones
    else:
        high, low = pieces(feats, 2)
        parts = [high, high, low] + ones + square
    used = 3 * width + 6
    parts.append(jnp.zeros((rows, -used % 256), BF16))
    return jnp.concatenate(parts, axis=1)


def paired(values):
    return jnp.concatenate(pieces(values, 2), axis=1)


def kmul_body(sub, tile, a_ref, b_ref, w_ref, o_ref):
    rows = a_ref.shape[0]
    wide = w_ref.shape[1]

    def step(index, totals):
        at = pl.ds(pl.multiple_of(index * tile, tile), tile)
        b = b_ref[at, :]
        w = w_ref[at, :]
        result = []
        for part in range(rows // sub):
            a = a_ref[pl.ds(part * sub, sub), :]
            expo = lax.dot_general(
                a, b, (((1,), (1,)), ((), ())), preferred_element_type=F32
            )
            value = jnp.exp2(expo)
            high = value.astype(BF16)
            low = (value - high.astype(F32)).astype(BF16)
            total = totals[part] + jnp.dot(high, w, preferred_element_type=F32)
            result.append(total + jnp.dot(low, w, preferred_element_type=F32))
        return tuple(result)

    zero = tuple(jnp.zeros((sub, wide), F32) for part in range(rows // sub))
    totals = lax.fori_loop(0, b_ref.shape[0] // tile, step, zero)
    for part, total in enumerate(totals):
        o_ref[pl.ds(part * sub, sub), :] = total[:, : wide // 2] + total[:, wide // 2 :]


def kmul(a, b, w, block=512, sub=256, tile=512):
    rows, deep = a.shape
    points, wide = w.shape
    block = min(block, rows)
    return pl.pallas_call(
        functools.partial(kmul_body, min(sub, block), min(tile, points)),
        out_shape=jax.ShapeDtypeStruct((rows, wide // 2), F32),
        grid=(rows // block,),
        in_specs=[
            pl.BlockSpec((block, deep), lambda i: (i, 0)),
            pl.BlockSpec((points, deep), lambda i: (0, 0)),
            pl.BlockSpec((points, wide), lambda i: (0, 0)),
        ],
        out_specs=pl.BlockSpec((block, wide // 2), lambda i: (i, 0)),
    )(a, b, w)


def pick_body(index_ref, cols_ref, o_ref):
    index = index_ref[0]
    rows = cols_ref.shape[1]
    spot = lax.broadcasted_iota(jnp.int32, (rows, index.shape[1]), 0)
    hot = jnp.where(spot == index, 1.0, 0.0).astype(BF16)
    got = jnp.dot(cols_ref[...], hot, preferred_element_type=F32)
    width = cols_ref.shape[0] // 3
    o_ref[0] = (got[:width] + got[width : 2 * width]) + got[2 * width :]


def pick(index, cols, width):
    blocks = index.shape[0]
    return pl.pallas_call(
        pick_body,
        out_shape=jax.ShapeDtypeStruct((blocks, width, 128), F32),
        grid=(blocks,),
        in_specs=[
            pl.BlockSpec((1, 1, 128), lambda i: (i, 0, 0)),
            pl.BlockSpec(cols.shape, lambda i: (0, 0)),
        ],
        out_specs=pl.BlockSpec((1, width, 128), lambda i: (i, 0, 0)),
    )(index, cols)


class Place:
    def __init__(self, xs, cs):
        self.xs, self.cs = xs, cs
        row = lax.axis_index("row")
        self.c = lax.axis_index("col")
        self.k = lax.rem(row, CORES)
        self.x = row // CORES

    def core(self):
        return [(1 - self.k, (self.x * CORES + 1 - self.k, self.c))]

    def line(self):
        spots = [lax.rem(self.x + d, self.xs) for d in range(1, self.xs)]
        return [(s, (s * CORES + self.k, self.c)) for s in spots]

    def cols(self):
        spots = [lax.rem(self.c + d, self.cs) for d in range(1, self.cs)]
        return [(s, (self.x * CORES + self.k, s)) for s in spots]

    def barrier(self):
        sem = pltpu.get_barrier_semaphore()
        everyone = self.core() + self.line() + self.cols()
        for spot, device in everyone:
            pl.semaphore_signal(sem, inc=1, device_id=device, device_id_type=MESH)
        pl.semaphore_wait(sem, len(everyone))


def exchange(partners, source, target, send, recv):
    copies = []
    for d, (spot, device) in enumerate(partners):
        copies.append(
            pltpu.make_async_remote_copy(
                src_ref=source(d, spot),
                dst_ref=target(d, spot),
                send_sem=send.at[d],
                recv_sem=recv.at[d],
                device_id=device,
                device_id_type=MESH,
            )
        )
    for copy in copies:
        copy.start()
    for copy in copies:
        copy.wait()


def summed(first, buffers, count):
    total = first
    for d in range(count):
        total = total + buffers[d]
    return total


def gather(place, o_ref, sems):
    k, x, c = place.k, place.x, place.c
    exchange(place.cols(), lambda d, s: o_ref.at[k, x, c], lambda d, s: o_ref.at[k, x, c], *sems[0])
    exchange(place.line(), lambda d, s: o_ref.at[k, x], lambda d, s: o_ref.at[k, x], *sems[1])
    exchange(place.core(), lambda d, s: o_ref.at[k], lambda d, s: o_ref.at[k], *sems[2])


def reduce_body(xs, cs, in_ref, o_ref, by_core, on_core, by_line, on_line, by_col, *sems):
    place = Place(xs, cs)
    sems = [sems[i : i + 2] for i in range(0, len(sems), 2)]
    place.barrier()
    exchange(place.core(), lambda d, s: in_ref.at[s], lambda d, s: by_core.at[d], *sems[0])
    on_core[...] = in_ref[place.k] + by_core[0]
    exchange(place.line(), lambda d, s: on_core.at[s], lambda d, s: by_line.at[d], *sems[1])
    on_line[...] = summed(on_core[place.x], by_line, xs - 1)
    exchange(place.cols(), lambda d, s: on_line.at[s], lambda d, s: by_col.at[d], *sems[2])
    o_ref[place.k, place.x, place.c] = summed(on_line[place.c], by_col, cs - 1)
    gather(place, o_ref, sems[3:])


def sem_list(counts):
    return [pltpu.SemaphoreType.DMA((n,)) for n in counts for both in range(2)]


def all_reduce(tiles, xs, cs, ident):
    count = tiles.shape[0]
    share = -(-count // (CORES * xs * cs))
    padded = jnp.pad(tiles, ((0, CORES * xs * cs * share - count), (0, 0), (0, 0)))
    piece = (share, 8, 128)
    whole = (CORES, xs, cs) + piece
    out = pl.pallas_call(
        functools.partial(reduce_body, xs, cs),
        out_shape=jax.ShapeDtypeStruct(whole, F32),
        in_specs=[VMEM],
        out_specs=VMEM,
        scratch_shapes=[
            pltpu.VMEM((1, xs, cs) + piece, F32),
            pltpu.VMEM((xs, cs) + piece, F32),
            pltpu.VMEM((xs - 1, cs) + piece, F32),
            pltpu.VMEM((cs,) + piece, F32),
            pltpu.VMEM((cs - 1,) + piece, F32),
        ]
        + sem_list([1, xs - 1, cs - 1, cs - 1, xs - 1, 1]),
        compiler_params=pltpu.CompilerParams(collective_id=ident, has_side_effects=True),
    )(padded.reshape(whole))
    return out.reshape((-1, 8, 128))[:count]


def modes_body(
    xs, cs, part_ref, scale_ref, eig_ref, o_ref,
    by_core, on_core, by_line, terms, by_col, *sems
):
    place = Place(xs, cs)
    sems = [sems[i : i + 2] for i in range(0, len(sems), 2)]
    place.barrier()
    exchange(place.core(), lambda d, s: part_ref, lambda d, s: by_core.at[d], *sems[0])
    on_core[...] = part_ref[...] + by_core[0]
    exchange(place.line(), lambda d, s: on_core, lambda d, s: by_line.at[d], *sems[1])
    coeff = summed(on_core[...], by_line, xs - 1) * scale_ref[...]
    share = eig_ref.shape[0] // cs
    for col in range(cs):
        terms[col] = lax.dot_general(
            coeff,
            eig_ref[pl.ds(col * share, share), :],
            (((1,), (1,)), ((), ())),
            precision=lax.Precision.HIGHEST,
            preferred_element_type=F32,
        )
    exchange(place.cols(), lambda d, s: terms.at[s], lambda d, s: by_col.at[d], *sems[2])
    o_ref[place.k, place.x, place.c] = summed(terms[place.c], by_col, cs - 1)
    gather(place, o_ref, sems[3:])


def corrections(part, scale, eigvecs, xs, cs, ident):
    outs, modes = part.shape
    share = eigvecs.shape[0] // cs
    out = pl.pallas_call(
        functools.partial(modes_body, xs, cs),
        out_shape=jax.ShapeDtypeStruct((CORES, xs, cs, outs, share), F32),
        in_specs=[VMEM] * 3,
        out_specs=VMEM,
        scratch_shapes=[
            pltpu.VMEM((1, outs, modes), F32),
            pltpu.VMEM((outs, modes), F32),
            pltpu.VMEM((xs - 1, outs, modes), F32),
            pltpu.VMEM((cs, outs, share), F32),
            pltpu.VMEM((cs - 1, outs, share), F32),
        ]
        + sem_list([1, xs - 1, cs - 1, cs - 1, xs - 1, 1]),
        compiler_params=pltpu.CompilerParams(collective_id=ident, has_side_effects=True),
    )(part, scale, eigvecs)
    return out.transpose(1, 0, 2, 4, 3).reshape((-1, outs))


def local(xs, cs, centres, weights, targets, batch_index, nystrom_index, eigvecs, mode_scale):
    rows_dev, width = centres.shape
    batch, outs = targets.shape
    block_rows = eigvecs.shape[0]
    offset = lax.axis_index(("row", "col")) * rows_dev

    index = jnp.concatenate([batch_index, nystrom_index]) - offset
    cols = jnp.concatenate(pieces(centres.T, 3), axis=0)
    mine = pick(index.reshape(-1, 1, 128), cols, width)
    feats = all_reduce(mine.reshape(-1, 8, 128), xs, cs, 0)
    feats = feats.reshape(-1, width, 128).transpose(0, 2, 1).reshape(-1, width)

    left = augmented(centres, True)
    right = augmented(feats, False)
    batch_left = augmented(feats[:batch], True)
    nys_block = lax.dynamic_slice_in_dim(
        right, batch + lax.axis_index("row") * block_rows, block_rows, 0
    )

    partial_pred = kmul(right[:batch], left, paired(weights))
    halves = jnp.concatenate([partial_pred[: batch // 2], partial_pred[batch // 2 :]], axis=1)
    summed_pred = all_reduce(halves.reshape(-1, 8, 128), xs, cs, 1).reshape(batch // 2, 2 * outs)
    prediction = jnp.concatenate([summed_pred[:, :outs], summed_pred[:, outs:]], axis=0)
    residual = prediction - targets

    gradient = kmul(nys_block, batch_left, paired(residual))
    part = lax.dot_general(
        gradient,
        eigvecs,
        (((0,), (0,)), ((), ())),
        precision=lax.Precision.HIGHEST,
        preferred_element_type=F32,
    )
    correction = corrections(part, mode_scale[None, :], eigvecs, xs, cs, 2)
    both = learning_rate * jnp.concatenate([residual, -correction], axis=0)
    step = kmul(left, right, paired(both))
    return (residual, step)


def solution(mesh):
    in_specs = (
        P(("row", "col"), None),
        P(("row", "col"), None),
        P(),
        P(),
        P(),
        P("row", "col"),
        P("col"),
    )
    out_specs = (P(), P(("row", "col"), None))
    body = functools.partial(local, mesh.shape["row"] // CORES, mesh.shape["col"])
    return jax.shard_map(body, mesh=mesh, in_specs=in_specs, out_specs=out_specs, check_vma=False)
```

```python
import functools
import math

import jax
import jax.numpy as jnp
from jax import lax
from jax.experimental import pallas as pl
from jax.experimental.pallas import tpu as pltpu
from jax.sharding import PartitionSpec as P

learning_rate = 0.25
CORES = 2
MESH = pl.DeviceIdType.MESH
VMEM = pl.BlockSpec(memory_space=pltpu.VMEM)
BF16 = jnp.bfloat16
F32 = jnp.float32


def pieces(value, count):
    parts = []
    for step in range(count):
        part = value.astype(BF16).astype(F32)
        parts.append(part)
        value = value - part
    return parts


def paired(value):
    return jnp.concatenate(pieces(value, 2), axis=0).astype(BF16)


def augmented(feats, left):
    width, count = feats.shape
    unit = math.log2(math.e) / width
    square = pieces(-unit * jnp.sum(feats * feats, axis=0, keepdims=True), 3)
    if left:
        high, low = pieces(feats * (2.0 * unit), 2)
        parts, first, one = [high, low, high], 0, 3
    else:
        high, low = pieces(feats, 2)
        parts, first, one = [high, high, low], 3, 0
    spot = lax.broadcasted_iota(jnp.int32, (8, count), 0)
    tail = jnp.where((spot >= one) & (spot < one + 3), 1.0, 0.0)
    for at, part in enumerate(square):
        tail = jnp.where(spot == first + at, part, tail)
    deep = depth_of(width)
    fill = jnp.zeros((deep - 3 * width - 8, count), F32)
    return jnp.concatenate(parts + [tail, fill], axis=0)


def depth_of(width):
    return -(-(3 * width + 8) // 128) * 128


def largest(count, limit):
    return max(d for d in range(1, limit + 1) if count % d == 0)


def kmul(a_ref, b_ref, w_ref, o_ref, finish):
    points, outs = a_ref.shape[0], o_ref.shape[0]
    wide = b_ref.shape[1]
    sub = min(512, points)
    parts = largest(points // sub, 3)
    tile = min(512, wide)

    def across(i, unused):
        to = pl.ds(pl.multiple_of(i * tile, tile), tile)
        b = b_ref[:, to]

        def down(j, total):
            for part in range(parts):
                at = pl.ds(pl.multiple_of((j * parts + part) * sub, sub), sub)
                value = jnp.exp2(jnp.dot(a_ref[at, :], b, preferred_element_type=F32))
                high = value.astype(BF16)
                low = (value - high.astype(F32)).astype(BF16)
                w = w_ref[:, at]
                total = total + (
                    jnp.dot(w, high, preferred_element_type=F32)
                    + jnp.dot(w, low, preferred_element_type=F32)
                )
            return total

        total = lax.fori_loop(0, points // (sub * parts), down, jnp.zeros((2 * outs, tile), F32))
        o_ref[:, to] = finish(total[:outs] + total[outs:], to)
        return unused

    lax.fori_loop(0, wide // tile, across, 0)


class Place:
    def __init__(self, xs, cs):
        self.xs, self.cs = xs, cs
        row = lax.axis_index("row")
        self.c = lax.axis_index("col")
        self.k = lax.rem(row, CORES)
        self.x = row // CORES

    def core(self):
        return [(1 - self.k, (self.x * CORES + 1 - self.k, self.c))]

    def line(self):
        spots = [lax.rem(self.x + d, self.xs) for d in range(1, self.xs)]
        return [(s, (s * CORES + self.k, self.c)) for s in spots]

    def cols(self):
        spots = [lax.rem(self.c + d, self.cs) for d in range(1, self.cs)]
        return [(s, (self.x * CORES + self.k, s)) for s in spots]

    def barrier(self):
        sem = pltpu.get_barrier_semaphore()
        everyone = self.core() + self.line() + self.cols()
        for spot, device in everyone:
            pl.semaphore_signal(sem, inc=1, device_id=device, device_id_type=MESH)
        pl.semaphore_wait(sem, len(everyone))


def start(partners, source, target, sems):
    copies = []
    for d, (spot, device) in enumerate(partners):
        copies.append(
            pltpu.make_async_remote_copy(
                src_ref=source(d, spot),
                dst_ref=target(d, spot),
                send_sem=sems[0].at[d],
                recv_sem=sems[1].at[d],
                device_id=device,
                device_id_type=MESH,
            )
        )
    for copy in copies:
        copy.start()
    return copies


def finish(copies):
    for copy in copies:
        copy.wait()


def summed(first, buffers, count):
    total = first
    for d in range(count):
        total = total + buffers[d]
    return total


def gather_steps(place, o_ref, sems):
    k, x, c = place.k, place.x, place.c
    copies = start(place.cols(), lambda d, s: o_ref.at[k, x, c], lambda d, s: o_ref.at[k, x, c], sems[0])
    yield
    finish(copies)
    copies = start(place.line(), lambda d, s: o_ref.at[k, x], lambda d, s: o_ref.at[k, x], sems[1])
    yield
    finish(copies)
    copies = start(place.core(), lambda d, s: o_ref.at[k], lambda d, s: o_ref.at[k], sems[2])
    yield
    finish(copies)


def reduce_steps(place, bufs, sems):
    in_ref, by_core, on_core, by_line, on_line, by_col, o_ref = bufs
    copies = start(place.core(), lambda d, s: in_ref.at[s], lambda d, s: by_core.at[d], sems[0])
    yield
    finish(copies)
    on_core[...] = in_ref[place.k] + by_core[0]
    copies = start(place.line(), lambda d, s: on_core.at[s], lambda d, s: by_line.at[d], sems[1])
    yield
    finish(copies)
    on_line[...] = summed(on_core[place.x], by_line, place.xs - 1)
    copies = start(place.cols(), lambda d, s: on_line.at[s], lambda d, s: by_col.at[d], sems[2])
    yield
    finish(copies)
    o_ref[place.k, place.x, place.c] = summed(on_line[place.c], by_col, place.cs - 1)
    yield from gather_steps(place, o_ref, sems[3:])


def mode_steps(place, bufs, sems, scale_ref, eig_ref):
    part, by_core, on_core, by_line, terms, by_col, o_ref = bufs
    copies = start(place.core(), lambda d, s: part, lambda d, s: by_core.at[d], sems[0])
    yield
    finish(copies)
    on_core[...] = part[...] + by_core[0]
    copies = start(place.line(), lambda d, s: on_core, lambda d, s: by_line.at[d], sems[1])
    yield
    finish(copies)
    coeff = summed(on_core[...], by_line, place.xs - 1) * scale_ref[...]
    correction = lax.dot_general(
        coeff,
        eig_ref[...],
        (((1,), (1,)), ((), ())),
        precision=lax.Precision.HIGHEST,
        preferred_element_type=F32,
    )
    store_tiles(correction, 0, lambda t, tile: place_in(terms, t, tile))
    copies = start(place.cols(), lambda d, s: terms.at[s], lambda d, s: by_col.at[d], sems[2])
    yield
    finish(copies)
    o_ref[place.k, place.x, place.c] = summed(terms[place.c], by_col, place.cs - 1)
    yield from gather_steps(place, o_ref, sems[3:])


def spot_of(shape, t):
    row, rest = divmod(t, shape[2] * shape[3])
    return (row % CORES, row // CORES) + divmod(rest, shape[3])


def place_in(terms, t, tile):
    terms[divmod(t, terms.shape[1])] = tile


def store_tiles(value, block, put):
    high = value.shape[0] // 8
    for j in range(value.shape[1] // 128):
        for g in range(high):
            put((block + j) * high + g, value[8 * g : 8 * g + 8, 128 * j : 128 * j + 128])


def store_all(buf, block, value):
    def put(t, tile):
        buf[spot_of(buf.shape, t)] = tile

    store_tiles(value, block, put)


def load_tiles(get, high, block, blocks):
    columns = []
    for j in range(block, block + blocks):
        columns.append(jnp.concatenate([get(j * high + g) for g in range(high)], axis=0))
    return jnp.concatenate(columns, axis=1) if blocks > 1 else columns[0]


def load_all(buf, high, block, blocks):
    return load_tiles(lambda t: buf[spot_of(buf.shape, t)], high, block, blocks)


def reduce_shapes(tiles, xs, cs):
    share = -(-tiles // (CORES * xs * cs))
    piece = (share, 8, 128)
    shapes = [
        (CORES, xs, cs) + piece,
        (1, xs, cs) + piece,
        (xs, cs) + piece,
        (xs - 1, cs) + piece,
        (cs,) + piece,
        (cs - 1,) + piece,
        (CORES, xs, cs) + piece,
    ]
    return [pltpu.VMEM(shape, F32) for shape in shapes]


CHUNK = 512


def main_body(
    xs, cs, batch, points, centres, weights, targets, index, scale, eig,
    residual, both, right, left, *scratch
):
    width, rows = centres.shape
    outs = targets.shape[0]
    high = width // 8
    b_bufs, n_bufs, p_bufs, m_bufs = (scratch[i : i + 7] for i in range(0, 28, 7))
    split, left_rows, batch_right, batch_left, block_right, pairs, pred, grad = scratch[28:36]
    sems = [scratch[i : i + 2] for i in range(36, len(scratch), 2)]
    place = Place(xs, cs)
    place.barrier()

    def pick(at, count):
        spot = lax.broadcasted_iota(jnp.int32, (rows, count), 0)
        hot = jnp.where(spot == index[:, at : at + count], 1.0, 0.0).astype(BF16)
        got = jnp.dot(split[...], hot, preferred_element_type=F32)
        return (got[:width] + got[width : 2 * width]) + got[2 * width :]

    def pick_points(first, last):
        for at in range(first, last, CHUNK):
            count = min(CHUNK, last - at)
            store_all(n_bufs[0], at // 128, pick(batch + at, count))

    def share(step, steps):
        size = -(-points // (steps * 128)) * 128
        return min(step * size, points), min(step * size + size, points)

    split[...] = jnp.concatenate(pieces(centres[...], 3), axis=0).astype(BF16)
    for bufs in (b_bufs, n_bufs, p_bufs, m_bufs):
        if bufs is not m_bufs:
            bufs[0][...] = jnp.zeros_like(bufs[0])
    for at in range(0, batch, CHUNK):
        store_all(b_bufs[0], at // 128, pick(at, min(CHUNK, batch - at)))
    of_batch = reduce_steps(place, b_bufs, sems[:6])
    of_points = reduce_steps(place, n_bufs, sems[6:12])
    next(of_batch)
    pick_points(*share(0, 4))
    next(of_batch)
    pick_points(*share(1, 4))
    next(of_batch)
    pick_points(*share(2, 4))
    pick_points(*share(3, 4))
    next(of_points)
    next(of_batch)
    for at in range(0, rows, CHUNK):
        to = slice(at, min(at + CHUNK, rows))
        form = augmented(centres[:, to], True)
        left[:, to] = form.astype(BF16)
        left_rows[to, :] = form.T.astype(BF16)
    pairs[...] = paired(weights[...])
    next(of_batch)
    next(of_points)
    next(of_batch)
    next(of_batch, None)

    feats = load_all(b_bufs[6], high, 0, batch // 128)
    form = augmented(feats, False)
    batch_right[...] = form.astype(BF16)
    kmul(left_rows, batch_right, pairs, pred, lambda total, to: total)
    store_all(p_bufs[0], 0, pred[...])
    of_pred = reduce_steps(place, p_bufs, sems[12:18])
    next(of_pred)
    right[:batch, :] = form.T.astype(BF16)
    batch_left[...] = augmented(feats, True).T.astype(BF16)
    next(of_pred)
    next(of_points)
    next(of_pred)
    next(of_pred)
    next(of_points)
    next(of_pred)
    next(of_pred)
    next(of_pred, None)

    rest = load_all(p_bufs[6], outs // 8, 0, batch // 128) - targets[...]
    residual[...] = rest
    both[:, :batch] = paired(learning_rate * rest)
    pairs_rest = paired(rest)
    next(of_points)
    mine = n_bufs[6].at[place.k, place.x]
    block = eig.shape[0]
    feats = load_tiles(lambda t: mine[divmod(t, mine.shape[1])], high, 0, block // 128)
    block_right[...] = augmented(feats, False).astype(BF16)
    pairs[:, :batch] = pairs_rest
    kmul(batch_left, block_right, pairs.at[:, :batch], grad, lambda total, to: total)
    m_bufs[0][...] = jnp.dot(
        grad[...], eig[...], precision=lax.Precision.HIGHEST, preferred_element_type=F32
    )
    of_modes = mode_steps(place, m_bufs, sems[18:24], scale, eig)

    def point_forms(first, last):
        for at in range(first, last, CHUNK):
            count = min(CHUNK, last - at)
            feats = load_all(n_bufs[6], high, at // 128, count // 128)
            right[batch + at : batch + at + count, :] = augmented(feats, False).T.astype(BF16)

    next(of_modes)
    next(of_modes)
    next(of_points)
    next(of_modes)
    next(of_points, None)
    point_forms(*share(0, 3))
    next(of_modes)
    point_forms(*share(1, 3))
    next(of_modes)
    point_forms(*share(2, 3))
    next(of_modes)
    next(of_modes, None)
    for at in range(0, points, CHUNK):
        count = min(CHUNK, points - at)
        correction = load_all(m_bufs[6], outs // 8, at // 128, count // 128)
        both[:, batch + at : batch + at + count] = paired(-learning_rate * correction)


def step_body(right, left, both, o_ref):
    kmul(right, left, both, o_ref, lambda total, to: total)


def local(xs, cs, centres, weights, targets, batch_index, nystrom_index, eigvecs, mode_scale):
    rows, width = centres.shape
    batch, outs = targets.shape
    points = nystrom_index.shape[0]
    block, modes = eigvecs.shape
    deep = depth_of(width)
    total = batch + points
    offset = lax.axis_index(("row", "col")) * rows
    index = jnp.concatenate([batch_index, nystrom_index])[None, :] - offset
    mode_share = -(-(outs // 8 * block // 128) // cs)
    piece = (mode_share, 8, 128)
    sums = [1, xs - 1, cs - 1, cs - 1, xs - 1, 1] * 4
    residual, both, right, left = pl.pallas_call(
        functools.partial(main_body, xs, cs, batch, points),
        out_shape=[
            jax.ShapeDtypeStruct((outs, batch), F32),
            jax.ShapeDtypeStruct((2 * outs, total), BF16),
            jax.ShapeDtypeStruct((total, deep), BF16),
            jax.ShapeDtypeStruct((deep, rows), BF16),
        ],
        in_specs=[VMEM] * 6,
        out_specs=[VMEM] * 4,
        scratch_shapes=reduce_shapes(width // 8 * batch // 128, xs, cs)
        + reduce_shapes(width // 8 * points // 128, xs, cs)
        + reduce_shapes(outs // 8 * batch // 128, xs, cs)
        + [
            pltpu.VMEM((outs, modes), F32),
            pltpu.VMEM((1, outs, modes), F32),
            pltpu.VMEM((outs, modes), F32),
            pltpu.VMEM((xs - 1, outs, modes), F32),
            pltpu.VMEM((cs,) + piece, F32),
            pltpu.VMEM((cs - 1,) + piece, F32),
            pltpu.VMEM((CORES, xs, cs) + piece, F32),
            pltpu.VMEM((3 * width, rows), BF16),
            pltpu.VMEM((rows, deep), BF16),
            pltpu.VMEM((deep, batch), BF16),
            pltpu.VMEM((batch, deep), BF16),
            pltpu.VMEM((deep, block), BF16),
            pltpu.VMEM((2 * outs, rows), BF16),
            pltpu.VMEM((outs, batch), F32),
            pltpu.VMEM((outs, block), F32),
        ]
        + [pltpu.SemaphoreType.DMA((n,)) for n in sums for both_ways in range(2)],
        compiler_params=pltpu.CompilerParams(collective_id=0, has_side_effects=True),
    )(centres.T, weights.T, targets.T, index, mode_scale[None, :], eigvecs)
    step = pl.pallas_call(
        step_body,
        out_shape=jax.ShapeDtypeStruct((outs, rows), F32),
        in_specs=[VMEM] * 3,
        out_specs=VMEM,
    )(right, left, both)
    return (residual.T, step.T)


def solution(mesh):
    in_specs = (
        P(("row", "col"), None),
        P(("row", "col"), None),
        P(),
        P(),
        P(),
        P("row", "col"),
        P("col"),
    )
    out_specs = (P(), P(("row", "col"), None))
    body = functools.partial(local, mesh.shape["row"] // CORES, mesh.shape["col"])
    return jax.shard_map(body, mesh=mesh, in_specs=in_specs, out_specs=out_specs, check_vma=False)
```
